32 devices in a mesh: seq: 8 (over z, x), head: 4 (over y, core).
Axes of the slice: x: 2, y: 2, z: 4, core: 2. Of those that a mesh axis runs over, the one named last changes fastest.
Arguments:
- query_rows: bfloat16 [2, 3072, 5120], P(None, ('seq', 'head')), may hold values from -27 to 27
- key_rows: bfloat16 [2, 3072, 5120], P(None, ('seq', 'head')), may hold values from -27 to 27
- value_rows: bfloat16 [2, 3072, 5120], P(None, ('seq', 'head')), may hold values from -6 to 6
- segment_ids: int32 [3072], replicated, may hold values from 0 to 3, never falling along the last dimension, each value on 1 to 1152 neighbouring positions
- query_gain: float32 [5120], replicated, may hold values from 0.1 to 1.9
- key_gain: float32 [5120], replicated, may hold values from 0.1 to 1.9
- guidance: int32 [4], replicated, may hold values from 4 to 32
Outputs:
- guided: bfloat16 [3072, 5120], P(('seq', 'head'))
The draws below stay inside these ranges and needn't reach their ends.
Inputs may be any that keep to these rules, and one draw needn't show every extreme that they name: `segment_ids`: segment numbers never fall along the rows; every clip 0 to 3 has 1 to 1152 rows, and some clip has exactly 1152 rows.
All inputs are finite; a program needn't handle non-finite values.
Results may differ from the reference program's by a relative error of at most 0.012.
The reference program's roundings to bfloat16 on the way count: a program that leaves them out, or rounds other values in their place, can miss the bound.
Values may be sent and summed in bfloat16 or wider, within the bound.
No kernel may reach another device: no remote copies, remote signals or barrier semaphores. Data moves between devices by JAX's collectives and lax.ppermute only.
A program may use at most 256 MiB of HBM per device.

```python
import math
import jax
import jax.numpy as jnp
import numpy as np
from jax import lax

D = 5120
HEAD_DIM = 128
R = 384
REACH = 3
TOKENS = 3072
CLIPS = 4
N_SEQ = 8


def draw_entries(key, which):
    own_key = jax.random.fold_in(key, 100 + which)
    column_scale = jnp.exp(jax.random.uniform(jax.random.fold_in(own_key, 1), (D,), jnp.float32, math.log(0.3), math.log(3.0)))
    row_scale = jnp.exp(jax.random.uniform(jax.random.fold_in(own_key, 2), (2, TOKENS, 1), jnp.float32, math.log(0.3), math.log(3.0)))
    normal_draw = jnp.clip(jax.random.normal(jax.random.fold_in(own_key, 5), (2, TOKENS, D), jnp.float32), -3.0, 3.0)
    return normal_draw * column_scale * row_scale


def draw_query_rows(key, part):
    return draw_entries(key, 0).astype(jnp.bfloat16)


def draw_key_rows(key, part):
    return draw_entries(key, 1).astype(jnp.bfloat16)


def with_ends(drawn, key, least, largest):
    place = [jax.random.randint(jax.random.fold_in(key, axis), (), 0, length) for axis, length in enumerate(drawn.shape)]
    longest = drawn.shape.index(max(drawn.shape))
    next_to = place[:longest] + [(place[longest] + 1) % drawn.shape[longest]] + place[longest + 1:]
    return drawn.at[tuple(place)].set(least).at[tuple(next_to)].set(largest)


def block_levels(stream_key, shape, cuts, low, high):
    def one(axis_at, blocks):
        heights = jax.random.uniform(jax.random.fold_in(jax.random.fold_in(stream_key, 6), axis_at), (blocks,), jnp.float32, low / len(cuts), high / len(cuts))
        return jnp.repeat(jnp.exp(heights), shape[axis_at] // blocks).reshape((-1,) + (1,) * (len(shape) - axis_at - 1))

    level = one(*cuts[0])
    for cut in cuts[1:]:
        level = level * one(*cut)
    return level


def profile(count, total, bound, slope):
    loads = [(1 << 20) // math.isqrt(grade ** slope) + 1 for grade in range(2, count + 1)]
    surplus, given = total - bound - (count - 1), [1] * (count - 1)
    while surplus > 0:
        free = [i for i in range(count - 1) if given[i] < bound]
        mass, left = sum([loads[i] for i in free]), surplus
        for i in free:
            extra = min(bound - given[i], max(1, left * loads[i] // mass), surplus)
            given[i] = given[i] + extra
            surplus = surplus - extra
    return np.array([bound] + given)


def uneven_parts(stream_key, count, total, most, lean):
    if count == 2:
        one = jax.random.randint(stream_key, (), max(1, total - most), min(most, total - 1) + 1)
        return jnp.stack([one, total - one])
    lengths = jnp.asarray(profile(count, total, most, lean), jnp.int32)
    twos = (count - 1) // 2
    donor, receiver = lengths[1:1 + 2 * twos:2], lengths[2:2 + 2 * twos:2]
    room = jnp.minimum(donor - 1, most - receiver)
    passed = jax.random.randint(jax.random.fold_in(stream_key, 1), (twos,), 0, 1 << 20) % (room + 1)
    lengths = lengths.at[1:1 + 2 * twos:2].set(donor - passed).at[2:2 + 2 * twos:2].set(receiver + passed)
    return lengths[jax.random.permutation(jax.random.fold_in(stream_key, 2), count)]


def normal_values(key, shape, deviation, most, split=(), kind=jnp.bfloat16):
    entries = jax.random.normal(key, shape, jnp.float32) * deviation
    if len(split) > 0:
        entries = block_levels(key, shape, split, -0.22, 0.18) * entries
    return jnp.clip(entries, min=-most, max=most).astype(kind)


def setup_inputs(seed: int = 0) -> dict:
    arg_keys = jax.random.split(jax.random.key(seed), 8)
    return {
        "query_rows": draw_query_rows(jax.random.fold_in(arg_keys[7], 71), 0),
        "key_rows": draw_key_rows(jax.random.fold_in(arg_keys[7], 71), 0),
        "value_rows": normal_values(arg_keys[2], (2, TOKENS, D), 1.0, 6.0, ((1, 32),)),
        "segment_ids": jnp.searchsorted(jnp.cumsum(uneven_parts(arg_keys[3], CLIPS, TOKENS, 3 * R, 2)), jnp.arange(TOKENS), side="right").astype(jnp.int32),
        "query_gain": jnp.clip(1.0 + 0.18 * jax.random.normal(arg_keys[4], (D,), jnp.float32), 0.1, 1.9),
        "key_gain": jnp.clip(1.0 + 0.18 * jax.random.normal(arg_keys[5], (D,), jnp.float32), 0.1, 1.9),
        "guidance": with_ends(jax.random.randint(arg_keys[6], (CLIPS,), 4, 33), jax.random.fold_in(arg_keys[6], 1), 4, 32).astype(jnp.int32),
    }


guide_denominator = 4.0
norm_epsilon = 1e-06
masked_score = -1e+30

def root_scale(raw_rows, gain):
    widened = raw_rows.astype(jnp.float32)
    mean_square = lax.optimization_barrier(jnp.mean(widened * widened, axis=-1, keepdims=True))
    return (widened * lax.rsqrt(mean_square + norm_epsilon) * gain).astype(jnp.bfloat16)

def reference(query_rows, key_rows, value_rows, segment_ids, query_gain, key_gain, guidance):
    branches, token_count, width = query_rows.shape
    head_count = width // HEAD_DIM
    margin = REACH * R
    window = (2 * REACH + 1) * R
    padded_keys = jnp.pad(key_rows, ((0, 0), (margin, margin), (0, 0)))
    padded_values = jnp.pad(value_rows, ((0, 0), (margin, margin), (0, 0)))
    padded_segments = jnp.pad(segment_ids, (margin, margin), constant_values=-1)

    def attend_block(block_index):
        first_row = (block_index * R).astype(jnp.int32)
        query_block = root_scale(lax.dynamic_slice_in_dim(query_rows, first_row, R, 1), query_gain)
        key_block = root_scale(lax.dynamic_slice_in_dim(padded_keys, first_row, window, 1), key_gain)
        value_block = lax.dynamic_slice_in_dim(padded_values, first_row, window, 1)
        query_segments = lax.dynamic_slice_in_dim(segment_ids, first_row, R)
        key_segments = lax.dynamic_slice_in_dim(padded_segments, first_row, window)
        query_heads = query_block.reshape(branches, R, head_count, HEAD_DIM).astype(jnp.float32)
        key_heads = key_block.reshape(branches, window, head_count, HEAD_DIM).astype(jnp.float32)
        value_heads = value_block.reshape(branches, window, head_count, HEAD_DIM).astype(jnp.float32)
        scores = jnp.einsum('bqhe,bkhe->bhqk', query_heads, key_heads) * HEAD_DIM ** (-0.5)
        same_clip = query_segments[:, None] == key_segments[None, :]
        scores = jnp.where(same_clip[None, None], scores, masked_score)
        row_max = lax.optimization_barrier(jnp.max(scores, axis=-1, keepdims=True))
        exponents = jnp.exp(scores - row_max)
        denominator = lax.optimization_barrier(jnp.sum(exponents, axis=-1))
        probs = exponents.astype(jnp.bfloat16).astype(jnp.float32)
        weighted = jnp.einsum('bhqk,bkhe->bqhe', probs, value_heads)
        attended = weighted / jnp.transpose(denominator, (0, 2, 1))[..., None]
        return attended.astype(jnp.bfloat16)
    blocks = lax.map(attend_block, jnp.arange(N_SEQ, dtype=jnp.int32))
    attended = jnp.transpose(blocks, (1, 0, 2, 3, 4)).reshape(branches, token_count, width)
    row_scale = guidance.astype(jnp.float32)[segment_ids] / guide_denominator
    uncond_rows = attended[1].astype(jnp.float32)
    cond_rows = attended[0].astype(jnp.float32)
    guided = uncond_rows + row_scale[:, None] * (cond_rows - uncond_rows)
    return guided.astype(jnp.bfloat16)
```

```python
import functools
import math

import jax
import jax.numpy as jnp
from jax import lax
from jax.experimental import pallas as pl
from jax.experimental.pallas import tpu as pltpu
from jax.sharding import PartitionSpec as P

HEAD_DIM = 128
REACH = 3
PAIR = 2
GROUPS = (2, 2, 1)

guide_denominator = 4.0
norm_epsilon = 1e-06
masked_score = -1e30
score_scale = HEAD_DIM ** (-0.5) * math.log2(math.e)
AXES = ("seq", "head")


def group_ranges(total):
    first, ranges = 0, []
    for count in GROUPS:
        ranges.append((first, count))
        first += count
    assert first == total
    return ranges


def normed(raw_rows, gain):
    widened = raw_rows.astype(jnp.float32)
    mean_square = jnp.mean(widened * widened, axis=-1, keepdims=True)
    return (widened * lax.rsqrt(mean_square + norm_epsilon) * gain).astype(jnp.bfloat16)


def scatter_heads(rows, out_refs, slot, parties):
    for ref in out_refs:
        width = ref.shape[-1]
        first = scatter_heads_start(out_refs, ref, parties)
        for party in range(parties):
            begin = first + party * width
            piece = rows[:, begin : begin + width]
            if slot is None:
                ref[party, 0] = piece
            else:
                ref[party, slot, 0] = piece


def scatter_heads_start(out_refs, ref, parties):
    first = 0
    for other in out_refs:
        if other is ref:
            return first
        first += other.shape[-1] * parties


def pack_keys_body(key_ref, value_ref, gain_ref, *out_refs, parties):
    scatter_heads(normed(key_ref[0], gain_ref[...]), out_refs, 0, parties)
    scatter_heads(value_ref[0], out_refs, 1, parties)


def pack_queries_body(query_ref, gain_ref, *out_refs, parties):
    scatter_heads(normed(query_ref[0], gain_ref[...]), out_refs, None, parties)


def pack(body, arrays, gain, parties, slots):
    branches, row_count, width = arrays[0].shape
    ranges = group_ranges(width // HEAD_DIM // parties)
    half = row_count // 2
    row_spec = pl.BlockSpec((1, half, width), lambda b, r: (b, r, 0))
    out_shape, out_specs = [], []
    for _, count in ranges:
        own = count * HEAD_DIM
        lead = (parties,) + slots
        out_shape.append(jax.ShapeDtypeStruct(lead + (branches, row_count, own), jnp.bfloat16))
        zeros = (0,) * len(lead)
        out_specs.append(
            pl.BlockSpec(lead + (1, half, own), lambda b, r, zeros=zeros: zeros + (b, r, 0))
        )
    return pl.pallas_call(
        functools.partial(body, parties=parties),
        grid=(branches, 2),
        in_specs=[row_spec] * len(arrays) + [pl.BlockSpec((1, width), lambda b, r: (0, 0))],
        out_specs=out_specs,
        out_shape=out_shape,
        compiler_params=pltpu.CompilerParams(vmem_limit_bytes=48 << 20),
    )(*arrays, gain.reshape(1, width))


def attend_body(active_ref, query_ref, *refs, tiles, chunks, chunk_refs):
    key_refs = refs[:chunk_refs]
    key_segments, query_segments, scale_ref, out_ref, max_ref, sum_ref, acc_ref = refs[chunk_refs:]
    branches = query_ref.shape[1]
    piece = query_ref.shape[2]
    for t, (tile_first, tile_pieces, home) in enumerate(tiles):
        tile_rows = tile_pieces * piece
        columns = slice(tile_first * piece, tile_first * piece + tile_rows)
        queries = [
            query_ref[tile_first : tile_first + tile_pieces, b].reshape(tile_rows, HEAD_DIM)
            for b in range(branches)
        ]
        own_segments = query_segments[:, columns]

        def absorb(c, first):
            which, begin, pieces, offset = chunks[c]
            rows = pieces * piece
            same = key_segments[offset * piece : offset * piece + rows, :1] == own_segments
            for b in range(branches):
                keys = key_refs[which][begin : begin + pieces, 0, b].reshape(rows, HEAD_DIM)
                values = key_refs[which][begin : begin + pieces, 1, b].reshape(rows, HEAD_DIM)
                scores = lax.dot_general(
                    keys, queries[b], (((1,), (1,)), ((), ())), preferred_element_type=jnp.float32
                )
                scores = jnp.where(same, scores * score_scale, masked_score)
                highest = jnp.max(scores, axis=0, keepdims=True)
                if not first:
                    old = max_ref[b]
                    highest = jnp.maximum(old, highest)
                    factor = jnp.exp2(old - highest)
                exponents = jnp.exp2(scores - highest)
                total = jnp.sum(exponents, axis=0, keepdims=True)
                product = lax.dot_general(
                    values,
                    exponents.astype(jnp.bfloat16),
                    (((0,), (0,)), ((), ())),
                    preferred_element_type=jnp.float32,
                )
                max_ref[b] = highest
                if first:
                    sum_ref[b] = total
                    acc_ref[b] = product
                else:
                    sum_ref[b] = sum_ref[b] * factor + total
                    acc_ref[b] = acc_ref[b] * factor + product

        absorb(home, True)
        for c in range(len(chunks)):
            if c != home:
                pl.when(active_ref[t * len(chunks) + c] != 0)(functools.partial(absorb, c, False))
        attended = [
            (acc_ref[b] / sum_ref[b]).astype(jnp.bfloat16).astype(jnp.float32)
            for b in range(branches)
        ]
        guided = attended[1] + scale_ref[:, columns] * (attended[0] - attended[1])
        guided = jnp.transpose(guided).astype(jnp.bfloat16)
        out_ref[tile_first : tile_first + tile_pieces] = guided.reshape(
            tile_pieces, piece, HEAD_DIM
        )


def attend(queries, key_arrays, plan, active, key_segments, query_segments, row_scale):
    tiles, chunks = plan
    parties, branches, piece, width = queries.shape
    head_count = width // HEAD_DIM
    plane_rows = parties * piece
    tile_rows = max(pieces for _, pieces, _ in tiles) * piece

    def head_spec(array):
        return pl.BlockSpec(
            array.shape[:-1] + (HEAD_DIM,), lambda h, _, n=array.ndim: (0,) * (n - 1) + (h,)
        )

    def whole_spec(array):
        return pl.BlockSpec(array.shape, lambda h, _, n=array.ndim: (0,) * n)

    return pl.pallas_call(
        functools.partial(attend_body, tiles=tiles, chunks=chunks, chunk_refs=len(key_arrays)),
        grid_spec=pltpu.PrefetchScalarGridSpec(
            num_scalar_prefetch=1,
            grid=(head_count,),
            in_specs=[head_spec(queries)]
            + [head_spec(array) for array in key_arrays]
            + [whole_spec(key_segments), whole_spec(query_segments), whole_spec(row_scale)],
            out_specs=pl.BlockSpec((parties, piece, HEAD_DIM), lambda h, _: (0, 0, h)),
            scratch_shapes=[
                pltpu.VMEM((branches, 1, tile_rows), jnp.float32),
                pltpu.VMEM((branches, 1, tile_rows), jnp.float32),
                pltpu.VMEM((branches, HEAD_DIM, tile_rows), jnp.float32),
            ],
        ),
        out_shape=jax.ShapeDtypeStruct((parties, piece, width), jnp.bfloat16),
        compiler_params=pltpu.CompilerParams(vmem_limit_bytes=48 << 20),
        cost_estimate=pl.CostEstimate(
            flops=4 * branches * plane_rows * plane_rows * width,
            transcendentals=branches * plane_rows * plane_rows * head_count,
            bytes_accessed=4 * branches * plane_rows * width * 2,
        ),
    )(active, queries, *key_arrays, key_segments, query_segments, row_scale)


def guide_rows(row_segments, guidance):
    clip_count = guidance.shape[0]
    one_hot = (row_segments[:, None] == jnp.arange(clip_count, dtype=jnp.int32)[None, :]).astype(
        jnp.float32
    )
    return (
        jnp.dot(one_hot, guidance.astype(jnp.float32), precision=lax.Precision.HIGHEST)
        / guide_denominator
    )


def on_device(query_rows, key_rows, value_rows, segment_ids, query_gain, key_gain, guidance):
    seq_count = lax.axis_size("seq")
    head_groups = lax.axis_size("head")
    parties = PAIR * head_groups
    planes = seq_count // PAIR
    plane = lax.axis_index("seq") // PAIR
    branches, piece, width = query_rows.shape
    plane_rows = parties * piece
    margin = REACH * head_groups * piece
    window_rows = plane_rows + 2 * margin
    half = head_groups

    padded = jnp.concatenate(
        [
            jnp.full((margin,), -1, jnp.int32),
            segment_ids,
            jnp.full((margin,), guidance.shape[0], jnp.int32),
        ]
    )
    window = lax.dynamic_slice_in_dim(padded, plane * plane_rows, window_rows)
    own_segments = lax.dynamic_slice_in_dim(segment_ids, plane * plane_rows, plane_rows)
    row_scale = guide_rows(own_segments, guidance)[None, :]
    key_segments = jnp.broadcast_to(window[:, None], (window_rows, HEAD_DIM))
    query_segments = own_segments[None, :]

    chunks = (
        (3, 0, half, 0),
        (2, 0, half, half),
        (1, 0, half, 2 * half),
        (0, 0, half, 3 * half),
        (0, half, half, 4 * half),
        (4, 0, half, 5 * half),
        (5, 0, half, 6 * half),
        (6, 0, half, 7 * half),
    )
    tiles = ((0, half, 3), (half, half, 4))
    chunk_first = jnp.stack([window[offset * piece] for _, _, _, offset in chunks])
    chunk_last = jnp.stack([window[(o + n) * piece - 1] for _, _, n, o in chunks])
    tile_first = jnp.stack([own_segments[f * piece] for f, _, _ in tiles])
    tile_last = jnp.stack([own_segments[(f + n) * piece - 1] for f, n, _ in tiles])
    active = jnp.logical_and(
        chunk_last[None, :] >= tile_first[:, None], chunk_first[None, :] <= tile_last[:, None]
    )
    active = active.astype(jnp.int32).reshape(-1)

    planes_of = [
        [plane_at * parties + member for member in range(parties)] for plane_at in range(planes)
    ]
    below = [(s, s + PAIR) for s in range(seq_count - PAIR)]
    above = [(s + PAIR, s) for s in range(seq_count - PAIR)]

    def exchange(array):
        return lax.all_to_all(array, AXES, 0, 0, axis_index_groups=planes_of, tiled=True)

    key_packs = pack(pack_keys_body, (key_rows, value_rows), key_gain, parties, (2,))
    query_packs = pack(pack_queries_body, (query_rows,), query_gain, parties, ())
    outputs = []
    for key_pack, query_pack in zip(key_packs, query_packs):
        own = exchange(key_pack)
        queries = exchange(query_pack)
        low, high = own[:half], own[half:]
        up_near = lax.ppermute(high, "seq", below)
        down_near = lax.ppermute(low, "seq", above)
        up_far = lax.ppermute(low, "seq", below)
        down_far = lax.ppermute(high, "seq", above)
        up_next = lax.ppermute(up_near, "seq", below)
        down_next = lax.ppermute(down_near, "seq", above)
        arrays = [own, up_near, up_far, up_next, down_near, down_far, down_next]
        attended = attend(
            queries, arrays, (tiles, chunks), active, key_segments, query_segments, row_scale
        )
        returned = exchange(attended)
        outputs.append(jnp.transpose(returned, (1, 0, 2)).reshape(piece, -1))
    return jnp.concatenate(outputs, axis=1)


def solution(mesh):
    placed = (
        P(None, ("seq", "head"), None),
        P(None, ("seq", "head"), None),
        P(None, ("seq", "head"), None),
        P(),
        P(),
        P(),
        P(),
    )
    return jax.shard_map(
        on_device, mesh=mesh, in_specs=placed, out_specs=P(("seq", "head"), None), check_vma=False
    )
```

```python
import functools
import math

import jax
import jax.numpy as jnp
from jax import lax
from jax.experimental import pallas as pl
from jax.experimental.pallas import tpu as pltpu
from jax.sharding import PartitionSpec as P

HEAD_DIM = 128
REACH = 3
PAIR = 2
GROUPS = (2, 2, 1)
TILE_KEYS = 640

guide_denominator = 4.0
norm_epsilon = 1e-06
masked_score = -1e30
score_scale = HEAD_DIM ** (-0.5) * math.log2(math.e)
AXES = ("seq", "head")


def group_ranges(total):
    first, ranges = 0, []
    for count in GROUPS:
        ranges.append((first, count))
        first += count
    assert first == total
    return ranges


def normed(raw_rows, gain):
    widened = raw_rows.astype(jnp.float32)
    mean_square = jnp.mean(widened * widened, axis=-1, keepdims=True)
    return (widened * lax.rsqrt(mean_square + norm_epsilon) * gain).astype(jnp.bfloat16)


def scatter_heads(rows, out_refs, slot, parties):
    for ref in out_refs:
        width = ref.shape[-1]
        first = scatter_heads_start(out_refs, ref, parties)
        for party in range(parties):
            begin = first + party * width
            piece = rows[:, begin : begin + width]
            ref[party, slot, 0] = piece


def scatter_heads_start(out_refs, ref, parties):
    first = 0
    for other in out_refs:
        if other is ref:
            return first
        first += other.shape[-1] * parties


def pack_keys_body(key_ref, value_ref, gain_ref, *out_refs, parties):
    scatter_heads(normed(key_ref[0], gain_ref[...]), out_refs, 0, parties)
    scatter_heads(value_ref[0], out_refs, 1, parties)


def pack_queries_body(query_ref, gain_ref, out_ref, *, parties):
    rows = normed(query_ref[0], gain_ref[...])
    for first, count in group_ranges(out_ref.shape[-1] // HEAD_DIM):
        width = count * HEAD_DIM
        for party in range(parties):
            begin = first * HEAD_DIM * parties + party * width
            out_ref[party, 0, :, first * HEAD_DIM : first * HEAD_DIM + width] = rows[:, begin : begin + width]


def pack(body, arrays, gain, parties, slots, ranges):
    branches, row_count, width = arrays[0].shape
    half = row_count // 2
    row_spec = pl.BlockSpec((1, half, width), lambda b, r: (b, r, 0))
    out_shape, out_specs = [], []
    for _, count in ranges:
        own = count * HEAD_DIM
        lead = (parties,) + slots
        out_shape.append(jax.ShapeDtypeStruct(lead + (branches, row_count, own), jnp.bfloat16))
        zeros = (0,) * len(lead)
        out_specs.append(
            pl.BlockSpec(lead + (1, half, own), lambda b, r, zeros=zeros: zeros + (b, r, 0))
        )
    return pl.pallas_call(
        functools.partial(body, parties=parties),
        grid=(branches, 2),
        in_specs=[row_spec] * len(arrays) + [pl.BlockSpec((1, width), lambda b, r: (0, 0))],
        out_specs=out_specs,
        out_shape=out_shape,
        compiler_params=pltpu.CompilerParams(vmem_limit_bytes=48 << 20),
    )(*arrays, gain.reshape(1, width))


def attend_body(bounds_ref, query_ref, *refs, chunks, chunk_refs, tile_rows, tile_keys):
    chunk_arrays = refs[:chunk_refs]
    key_segments, query_segments, scale_ref, out_ref = refs[chunk_refs : chunk_refs + 4]
    query_rows, key_rows, value_rows, max_ref, sum_ref, acc_ref = refs[chunk_refs + 4 :]
    parties, branches, piece, _ = query_ref.shape
    plane_rows = parties * piece
    tiles = plane_rows // tile_rows
    every = range(branches)
    lowest = bounds_ref[0]
    beyond = bounds_ref[2 * tiles - 1]

    @pl.when(pl.program_id(0) == 0)
    def _():
        value_rows[...] = jnp.zeros(value_rows.shape, value_rows.dtype)

    for b in every:
        query_rows[b] = query_ref[:, b].reshape(plane_rows, HEAD_DIM)
    for which, begin, pieces, offset in chunks:
        rows = pieces * piece
        first = offset * piece

        @pl.when(jnp.logical_and(first < beyond, first + rows > lowest))
        def _():
            for b in every:
                here = chunk_arrays[which][begin : begin + pieces, :, b]
                key_rows[b, first : first + rows] = here[:, 0].reshape(rows, HEAD_DIM)
                value_rows[b, first : first + rows] = here[:, 1].reshape(rows, HEAD_DIM)

    def attend_tile(t, _):
        at = pl.ds(pl.multiple_of(t * tile_rows, tile_rows), tile_rows)
        start = bounds_ref[2 * t] // HEAD_DIM * HEAD_DIM
        count = (bounds_ref[2 * t + 1] - start + tile_keys - 1) // tile_keys
        own_segments = query_segments[at]
        queries = [query_rows[b, at] for b in every]
        for b in every:
            max_ref[b] = jnp.full((tile_rows, HEAD_DIM), masked_score, jnp.float32)
            sum_ref[b] = jnp.zeros((tile_rows, HEAD_DIM), jnp.float32)
            acc_ref[b] = jnp.zeros((tile_rows, HEAD_DIM), jnp.float32)

        def absorb(k, _):
            here = pl.ds(pl.multiple_of(start + k * tile_keys, HEAD_DIM), tile_keys)
            copies = tile_keys // HEAD_DIM
            same = jnp.concatenate([own_segments] * copies, axis=1) == key_segments[:, here]
            old = [max_ref[b] for b in every]
            sums = [sum_ref[b] for b in every]
            weighted = [acc_ref[b] for b in every]
            keys = [key_rows[b, here] for b in every]
            values = [value_rows[b, here] for b in every]
            scores = [
                lax.dot_general(
                    queries[b], keys[b], (((1,), (1,)), ((), ())), preferred_element_type=jnp.float32
                )
                for b in every
            ]
            scores = [jnp.where(same, scores[b] * score_scale, masked_score) for b in every]
            highest = [
                jnp.maximum(old[b], jnp.max(scores[b], axis=1, keepdims=True)) for b in every
            ]
            factor = [jnp.exp2(old[b] - highest[b]) for b in every]
            exponents = [
                jnp.exp2(scores[b] - jnp.concatenate([highest[b]] * copies, axis=1)) for b in every
            ]
            partial = []
            for b in every:
                lanes = exponents[b][:, :HEAD_DIM]
                for i in range(1, copies):
                    lanes = lanes + exponents[b][:, i * HEAD_DIM : (i + 1) * HEAD_DIM]
                partial.append(lanes)
            products = [
                jnp.dot(
                    exponents[b].astype(jnp.bfloat16), values[b], preferred_element_type=jnp.float32
                )
                for b in every
            ]
            for b in every:
                max_ref[b] = highest[b]
                sum_ref[b] = sums[b] * factor[b] + partial[b]
                acc_ref[b] = weighted[b] * factor[b] + products[b]
            return 0

        lax.fori_loop(0, count, absorb, 0)
        attended = [
            (acc_ref[b] / jnp.sum(sum_ref[b], axis=1, keepdims=True))
            .astype(jnp.bfloat16)
            .astype(jnp.float32)
            for b in every
        ]
        guided = attended[1] + scale_ref[at] * (attended[0] - attended[1])
        out_ref[at] = guided.astype(jnp.bfloat16)
        return 0

    lax.fori_loop(0, tiles, attend_tile, 0)


def attend(queries, first_head, key_arrays, chunks, frame):
    bounds, key_segments, query_segments, row_scale = frame
    parties, branches, piece, _ = queries.shape
    width = key_arrays[0].shape[-1]
    plane_rows = parties * piece
    tiles = bounds.shape[0] // 2
    window_rows = key_segments.shape[1]

    def head_spec(array, skip):
        return pl.BlockSpec(
            array.shape[:-1] + (HEAD_DIM,),
            lambda h, _, n=array.ndim, skip=skip: (0,) * (n - 1) + (h + skip,),
        )

    def whole_spec(array):
        return pl.BlockSpec(array.shape, lambda h, _, n=array.ndim: (0,) * n)

    tile_rows = plane_rows // tiles
    return pl.pallas_call(
        functools.partial(
            attend_body,
            chunks=chunks,
            chunk_refs=len(key_arrays),
            tile_rows=tile_rows,
            tile_keys=TILE_KEYS,
        ),
        grid_spec=pltpu.PrefetchScalarGridSpec(
            num_scalar_prefetch=1,
            grid=(width // HEAD_DIM,),
            in_specs=[head_spec(queries, first_head)]
            + [head_spec(array, 0) for array in key_arrays]
            + [whole_spec(key_segments), whole_spec(query_segments), whole_spec(row_scale)],
            out_specs=pl.BlockSpec((plane_rows, HEAD_DIM), lambda h, _: (0, h)),
            scratch_shapes=[
                pltpu.VMEM((branches, plane_rows, HEAD_DIM), jnp.bfloat16),
                pltpu.VMEM((branches, window_rows, HEAD_DIM), jnp.bfloat16),
                pltpu.VMEM((branches, window_rows, HEAD_DIM), jnp.bfloat16),
                pltpu.VMEM((branches, tile_rows, HEAD_DIM), jnp.float32),
                pltpu.VMEM((branches, tile_rows, HEAD_DIM), jnp.float32),
                pltpu.VMEM((branches, tile_rows, HEAD_DIM), jnp.float32),
            ],
        ),
        out_shape=jax.ShapeDtypeStruct((plane_rows, width), jnp.bfloat16),
        compiler_params=pltpu.CompilerParams(vmem_limit_bytes=48 << 20),
        cost_estimate=pl.CostEstimate(
            flops=4 * branches * plane_rows * plane_rows * width,
            transcendentals=branches * plane_rows * plane_rows * width // HEAD_DIM,
            bytes_accessed=4 * branches * plane_rows * width * 2,
        ),
    )(bounds, queries, *key_arrays, key_segments, query_segments, row_scale)


def guide_rows(row_segments, guidance):
    clip_count = guidance.shape[0]
    one_hot = (row_segments[:, None] == jnp.arange(clip_count, dtype=jnp.int32)[None, :]).astype(
        jnp.float32
    )
    return (
        jnp.dot(one_hot, guidance.astype(jnp.float32), precision=lax.Precision.HIGHEST)
        / guide_denominator
    )


def after(value, *gates):
    return lax.optimization_barrier((value,) + gates)[0]


def on_device(query_rows, key_rows, value_rows, segment_ids, query_gain, key_gain, guidance):
    seq_count = lax.axis_size("seq")
    head_groups = lax.axis_size("head")
    parties = PAIR * head_groups
    planes = seq_count // PAIR
    plane = lax.axis_index("seq") // PAIR
    branches, piece, width = query_rows.shape
    plane_rows = parties * piece
    margin = REACH * head_groups * piece
    window_rows = plane_rows + 2 * margin
    half = head_groups

    rows = jnp.arange(window_rows + TILE_KEYS, dtype=jnp.int32) + (plane * plane_rows - margin)
    padded = jnp.pad(segment_ids, (margin, margin + TILE_KEYS))
    window = lax.dynamic_slice_in_dim(padded, plane * plane_rows, window_rows + TILE_KEYS)
    window = jnp.where(rows < 0, -1, jnp.where(rows < segment_ids.shape[0], window, guidance.shape[0]))
    own_segments = lax.dynamic_slice_in_dim(segment_ids, plane * plane_rows, plane_rows)
    row_scale = jnp.broadcast_to(guide_rows(own_segments, guidance)[:, None], (plane_rows, HEAD_DIM))
    tile_segments = own_segments.reshape(PAIR, plane_rows // PAIR)
    ends = jnp.stack([tile_segments[:, 0] - 1, tile_segments[:, -1]], axis=1).reshape(-1, 1)
    bounds = jnp.sum((window[None, :] <= ends).astype(jnp.int32), axis=1)
    frame = (
        bounds,
        window[None, :],
        jnp.broadcast_to(own_segments[:, None], (plane_rows, HEAD_DIM)),
        row_scale,
    )

    chunks = (
        (0, 0, parties, 3 * half),
        (1, 0, parties, half),
        (2, 0, parties, 5 * half),
        (3, 0, half, 0),
        (4, 0, half, 7 * half),
    )
    planes_of = [
        [plane_at * parties + member for member in range(parties)] for plane_at in range(planes)
    ]
    below = [(s, s + PAIR) for s in range(seq_count - PAIR)]
    above = [(s + PAIR, s) for s in range(seq_count - PAIR)]

    def exchange(array):
        return lax.all_to_all(array, AXES, 0, 0, axis_index_groups=planes_of, tiled=True)

    def shift(up, down):
        return lax.ppermute(up, "seq", below), lax.ppermute(down, "seq", above)

    heads = width // HEAD_DIM // parties
    ranges = group_ranges(heads)
    key_packs = pack(pack_keys_body, (key_rows, value_rows), key_gain, parties, (2,), ranges)
    (query_pack,) = pack(pack_queries_body, (query_rows,), query_gain, parties, (), [(0, heads)])
    first_own = exchange(key_packs[0])
    last_group = len(GROUPS) - 1

    def finish(own, later_packs, query_pack, frame, far):
        owns, fulls, nexts, attended = [own], [], [], []
        queries = None
        for g in range(len(GROUPS)):
            if g == 1:
                owns.append(exchange(later_packs[0]))
                queries = exchange(after(query_pack, owns[1]))
            elif g > 1:
                owns.append(exchange(after(later_packs[g - 1], queries)))
            full = (owns[g], owns[g])
            if g > 0:
                full = after(full, fulls[g - 1])
            if g == last_group and not far:
                full = after(full, *attended)
            fulls.append(shift(*full))
            if far:
                following = (fulls[g][0][half:], fulls[g][1][:half])
                if g == last_group:
                    following = after(following, *attended)
                nexts.append(shift(*following))
            else:
                nexts.append(())
            if 0 < g:
                attended.append(meet(queries, g - 1, owns, fulls, nexts, frame))
        attended.append(meet(queries, last_group, owns, fulls, nexts, frame))
        outputs = []
        for g in range(len(GROUPS)):
            returned = exchange(attended[g].reshape(parties, piece, -1))
            outputs.append(jnp.transpose(returned, (1, 0, 2)).reshape(piece, -1))
        return jnp.concatenate(outputs, axis=1)

    def meet(queries, g, owns, fulls, nexts, frame):
        arrays = [owns[g], *fulls[g], *nexts[g]]
        return attend(queries, ranges[g][0], arrays, chunks[: len(arrays)], frame)

    operands = (first_own, key_packs[1:], query_pack, frame)
    near_only = functools.partial(finish, far=False)
    if planes < 3:
        return near_only(*operands)
    bounding = segment_ids.reshape(planes, plane_rows)
    crossed = jnp.any(bounding[:-2, -1] == bounding[2:, 0])
    return lax.cond(crossed, functools.partial(finish, far=True), near_only, *operands)


def solution(mesh):
    placed = (
        P(None, ("seq", "head"), None),
        P(None, ("seq", "head"), None),
        P(None, ("seq", "head"), None),
        P(),
        P(),
        P(),
        P(),
    )
    return jax.shard_map(
        on_device, mesh=mesh, in_specs=placed, out_specs=P(("seq", "head"), None), check_vma=False
    )
```

```python
import functools
import math

import jax
import jax.numpy as jnp
from jax import lax
from jax.experimental import pallas as pl
from jax.experimental.pallas import tpu as pltpu
from jax.sharding import PartitionSpec as P

HEAD_DIM = 128
REACH = 3
PAIR = 2
GROUPS = (2, 2, 1)
TILE_KEYS = 1280

guide_denominator = 4.0
norm_epsilon = 1e-06
masked_score = -1e30
score_scale = HEAD_DIM ** (-0.5) * math.log2(math.e)
AXES = ("seq", "head")


def group_ranges(total):
    first, ranges = 0, []
    for count in GROUPS:
        ranges.append((first, count))
        first += count
    assert first == total
    return ranges


def return_of(group):
    bounds = (0, sum(GROUPS[:-1]), sum(GROUPS))
    which = 0 if group < len(GROUPS) - 1 else 1
    return bounds[which], bounds[which + 1] - bounds[which]


def first_feature(group, party, parties):
    first, count = return_of(group)
    own = sum(GROUPS[:group]) - first
    return (first * parties + party * count + own) * HEAD_DIM


def normed(raw_rows, gain):
    widened = raw_rows.astype(jnp.float32)
    mean_square = jnp.mean(widened * widened, axis=-1, keepdims=True)
    return (widened * lax.rsqrt(mean_square + norm_epsilon) * gain).astype(jnp.bfloat16)


def scatter_heads(rows, out_refs, slot, parties):
    for group, ref in enumerate(out_refs):
        for party in range(parties):
            begin = first_feature(group, party, parties)
            ref[party, slot, 0] = rows[:, begin : begin + ref.shape[-1]]


def pack_keys_body(key_ref, value_ref, gain_ref, *out_refs, parties):
    scatter_heads(normed(key_ref[0], gain_ref[...]), out_refs, 0, parties)
    scatter_heads(value_ref[0], out_refs, 1, parties)


def pack_queries_body(query_ref, gain_ref, out_ref, *, parties):
    rows = normed(query_ref[0], gain_ref[...])
    for group, (first, count) in enumerate(group_ranges(out_ref.shape[-1] // HEAD_DIM)):
        columns = slice(first * HEAD_DIM, (first + count) * HEAD_DIM)
        for party in range(parties):
            begin = first_feature(group, party, parties)
            out_ref[party, 0, :, columns] = rows[:, begin : begin + count * HEAD_DIM]


def pack(body, arrays, gain, parties, slots, ranges):
    branches, row_count, width = arrays[0].shape
    half = row_count // 2
    row_spec = pl.BlockSpec((1, half, width), lambda b, r: (b, r, 0))
    out_shape, out_specs = [], []
    for _, count in ranges:
        own = count * HEAD_DIM
        lead = (parties,) + slots
        out_shape.append(jax.ShapeDtypeStruct(lead + (branches, row_count, own), jnp.bfloat16))
        zeros = (0,) * len(lead)
        out_specs.append(
            pl.BlockSpec(lead + (1, half, own), lambda b, r, zeros=zeros: zeros + (b, r, 0))
        )
    return pl.pallas_call(
        functools.partial(body, parties=parties),
        grid=(branches, 2),
        in_specs=[row_spec] * len(arrays) + [pl.BlockSpec((1, width), lambda b, r: (0, 0))],
        out_specs=out_specs,
        out_shape=out_shape,
        compiler_params=pltpu.CompilerParams(vmem_limit_bytes=48 << 20),
    )(*arrays, gain.reshape(1, width))


def attend_body(bounds_ref, query_ref, *refs, chunks, chunk_refs, tile_rows, tile_keys):
    chunk_arrays = refs[:chunk_refs]
    key_segments, query_segments, scale_ref = refs[chunk_refs : chunk_refs + 3]
    out_ref, query_rows, key_rows, value_rows, max_ref, sum_ref, acc_ref = refs[-7:]
    parties, branches, piece, _ = query_ref.shape
    plane_rows = parties * piece
    tiles = plane_rows // tile_rows
    every = range(branches)
    lowest = bounds_ref[0]
    beyond = bounds_ref[2 * tiles - 1]

    @pl.when(pl.program_id(0) == 0)
    def _():
        value_rows[...] = jnp.zeros(value_rows.shape, value_rows.dtype)

    for b in every:
        query_rows[b] = query_ref[:, b].reshape(plane_rows, HEAD_DIM)
    for which, begin, pieces, offset in chunks:
        rows = pieces * piece
        first = offset * piece

        @pl.when(jnp.logical_and(first < beyond, first + rows > lowest))
        def _():
            for b in every:
                here = chunk_arrays[which][begin : begin + pieces, :, b]
                key_rows[b, first : first + rows] = here[:, 0].reshape(rows, HEAD_DIM)
                value_rows[b, first : first + rows] = here[:, 1].reshape(rows, HEAD_DIM)

    def attend_tile(t, _):
        at = pl.ds(pl.multiple_of(t * tile_rows, tile_rows), tile_rows)
        start = bounds_ref[2 * t] // HEAD_DIM * HEAD_DIM
        count = (bounds_ref[2 * t + 1] - start + tile_keys - 1) // tile_keys
        own_segments = query_segments[at]
        queries = [query_rows[b, at] for b in every]
        for b in every:
            max_ref[b] = jnp.full((tile_rows, HEAD_DIM), masked_score, jnp.float32)
            sum_ref[b] = jnp.zeros((tile_rows, HEAD_DIM), jnp.float32)
            acc_ref[b] = jnp.zeros((tile_rows, HEAD_DIM), jnp.float32)

        def absorb(k, _):
            here = pl.ds(pl.multiple_of(start + k * tile_keys, HEAD_DIM), tile_keys)
            copies = tile_keys // HEAD_DIM
            same = jnp.concatenate([own_segments] * copies, axis=1) == key_segments[:, here]
            old = [max_ref[b] for b in every]
            sums = [sum_ref[b] for b in every]
            weighted = [acc_ref[b] for b in every]
            keys = [key_rows[b, here] for b in every]
            values = [value_rows[b, here] for b in every]
            scores = [
                lax.dot_general(
                    queries[b], keys[b], (((1,), (1,)), ((), ())), preferred_element_type=jnp.float32
                )
                for b in every
            ]
            scores = [jnp.where(same, scores[b] * score_scale, masked_score) for b in every]
            highest = [
                jnp.maximum(old[b], jnp.max(scores[b], axis=1, keepdims=True)) for b in every
            ]
            factor = [jnp.exp2(old[b] - highest[b]) for b in every]
            exponents = [
                jnp.exp2(scores[b] - jnp.concatenate([highest[b]] * copies, axis=1)) for b in every
            ]
            partial = []
            for b in every:
                lanes = exponents[b][:, :HEAD_DIM]
                for i in range(1, copies):
                    lanes = lanes + exponents[b][:, i * HEAD_DIM : (i + 1) * HEAD_DIM]
                partial.append(lanes)
            products = [
                jnp.dot(
                    exponents[b].astype(jnp.bfloat16), values[b], preferred_element_type=jnp.float32
                )
                for b in every
            ]
            for b in every:
                max_ref[b] = highest[b]
                sum_ref[b] = sums[b] * factor[b] + partial[b]
                acc_ref[b] = weighted[b] * factor[b] + products[b]
            return 0

        lax.fori_loop(0, count, absorb, 0)
        attended = [
            (acc_ref[b] / jnp.sum(sum_ref[b], axis=1, keepdims=True))
            .astype(jnp.bfloat16)
            .astype(jnp.float32)
            for b in every
        ]
        guided = attended[1] + scale_ref[at] * (attended[0] - attended[1])
        out_ref[at] = guided.astype(jnp.bfloat16)
        return 0

    lax.fori_loop(0, tiles, attend_tile, 0)


def attend(queries, first_head, key_arrays, chunks, frame, out_heads, out_first, into):
    bounds, key_segments, query_segments, row_scale = frame
    parties, branches, piece, _ = queries.shape
    width = key_arrays[0].shape[-1]
    plane_rows = parties * piece
    tiles = bounds.shape[0] // 2
    window_rows = key_segments.shape[1]

    def head_spec(array, skip):
        return pl.BlockSpec(
            array.shape[:-1] + (HEAD_DIM,),
            lambda h, _, n=array.ndim, skip=skip: (0,) * (n - 1) + (h + skip,),
        )

    def whole_spec(array):
        return pl.BlockSpec(array.shape, lambda h, _, n=array.ndim: (0,) * n)

    tile_rows = plane_rows // tiles
    return pl.pallas_call(
        functools.partial(
            attend_body,
            chunks=chunks,
            chunk_refs=len(key_arrays),
            tile_rows=tile_rows,
            tile_keys=TILE_KEYS,
        ),
        grid_spec=pltpu.PrefetchScalarGridSpec(
            num_scalar_prefetch=1,
            grid=(width // HEAD_DIM,),
            in_specs=[head_spec(queries, first_head)]
            + [head_spec(array, 0) for array in key_arrays]
            + [whole_spec(key_segments), whole_spec(query_segments), whole_spec(row_scale)]
            + [pl.BlockSpec(memory_space=pl.ANY)] * len(into),
            out_specs=pl.BlockSpec((plane_rows, HEAD_DIM), lambda h, _: (0, h + out_first)),
            scratch_shapes=[
                pltpu.VMEM((branches, plane_rows, HEAD_DIM), jnp.bfloat16),
                pltpu.VMEM((branches, window_rows, HEAD_DIM), jnp.bfloat16),
                pltpu.VMEM((branches, window_rows, HEAD_DIM), jnp.bfloat16),
                pltpu.VMEM((branches, tile_rows, HEAD_DIM), jnp.float32),
                pltpu.VMEM((branches, tile_rows, HEAD_DIM), jnp.float32),
                pltpu.VMEM((branches, tile_rows, HEAD_DIM), jnp.float32),
            ],
        ),
        out_shape=jax.ShapeDtypeStruct((plane_rows, out_heads * HEAD_DIM), jnp.bfloat16),
        input_output_aliases={5 + len(key_arrays): 0} if into else {},
        compiler_params=pltpu.CompilerParams(vmem_limit_bytes=48 << 20),
        cost_estimate=pl.CostEstimate(
            flops=4 * branches * plane_rows * plane_rows * width,
            transcendentals=branches * plane_rows * plane_rows * width // HEAD_DIM,
            bytes_accessed=4 * branches * plane_rows * width * 2,
        ),
    )(bounds, queries, *key_arrays, key_segments, query_segments, row_scale, *into)


def guide_rows(row_segments, guidance):
    clip_count = guidance.shape[0]
    one_hot = (row_segments[:, None] == jnp.arange(clip_count, dtype=jnp.int32)[None, :]).astype(
        jnp.float32
    )
    return (
        jnp.dot(one_hot, guidance.astype(jnp.float32), precision=lax.Precision.HIGHEST)
        / guide_denominator
    )


def after(value, *gates):
    return lax.optimization_barrier((value,) + gates)[0]


def on_device(query_rows, key_rows, value_rows, segment_ids, query_gain, key_gain, guidance):
    seq_count = lax.axis_size("seq")
    head_groups = lax.axis_size("head")
    parties = PAIR * head_groups
    planes = seq_count // PAIR
    plane = lax.axis_index("seq") // PAIR
    branches, piece, width = query_rows.shape
    plane_rows = parties * piece
    margin = REACH * head_groups * piece
    window_rows = plane_rows + 2 * margin
    half = head_groups

    rows = jnp.arange(window_rows + TILE_KEYS, dtype=jnp.int32) + (plane * plane_rows - margin)
    padded = jnp.pad(segment_ids, (margin, margin + TILE_KEYS))
    window = lax.dynamic_slice_in_dim(padded, plane * plane_rows, window_rows + TILE_KEYS)
    window = jnp.where(rows < 0, -1, jnp.where(rows < segment_ids.shape[0], window, guidance.shape[0]))
    own_segments = lax.dynamic_slice_in_dim(segment_ids, plane * plane_rows, plane_rows)
    row_scale = jnp.broadcast_to(guide_rows(own_segments, guidance)[:, None], (plane_rows, HEAD_DIM))
    tile_segments = own_segments.reshape(PAIR, plane_rows // PAIR)
    ends = jnp.stack([tile_segments[:, 0] - 1, tile_segments[:, -1]], axis=1).reshape(-1, 1)
    bounds = jnp.sum((window[None, :] <= ends).astype(jnp.int32), axis=1)
    frame = (
        bounds,
        window[None, :],
        jnp.broadcast_to(own_segments[:, None], (plane_rows, HEAD_DIM)),
        row_scale,
    )

    chunks = (
        (0, 0, parties, 3 * half),
        (1, 0, parties, half),
        (2, 0, parties, 5 * half),
        (3, 0, half, 0),
        (4, 0, half, 7 * half),
    )
    planes_of = [
        [plane_at * parties + member for member in range(parties)] for plane_at in range(planes)
    ]
    below = [(s, s + PAIR) for s in range(seq_count - PAIR)]
    above = [(s + PAIR, s) for s in range(seq_count - PAIR)]

    def exchange(array):
        return lax.all_to_all(array, AXES, 0, 0, axis_index_groups=planes_of, tiled=True)

    heads = width // HEAD_DIM // parties
    ranges = group_ranges(heads)
    key_packs = pack(pack_keys_body, (key_rows, value_rows), key_gain, parties, (2,), ranges)
    (query_pack,) = pack(pack_queries_body, (query_rows,), query_gain, parties, (), [(0, heads)])
    first_own = exchange(key_packs[0])
    last_group = len(GROUPS) - 1

    def finish(own, later_packs, query_pack, frame, far):
        owns, queries = [own], None
        previous = []
        for step in (1, -1, 2):
            if step < 0:
                queries = exchange(after(query_pack, *previous))
                previous = [queries]
            else:
                owns.append(exchange(after(later_packs[step - 1], *previous)))
                previous = [owns[-1]]
        ups, downs, arrays = [], [], []
        met = []

        def meet(g):
            first, count = ranges[g]
            out_first, out_heads = return_of(g)
            into = met[-1:] if first > out_first else []
            met.append(
                attend(
                    queries, first, arrays[g], chunks[: len(arrays[g])], frame,
                    out_heads, first - out_first, into,
                )
            )

        for g in range(len(GROUPS)):
            up = down = owns[g]
            if g > 0:
                up, down = after(up, ups[g - 1]), after(down, downs[g - 1])
            if g == last_group and not far:
                for earlier in range(1):
                    meet(earlier)
                up, down = after(up, *met), after(down, *met)
            ups.append(lax.ppermute(up, "seq", below))
            downs.append(lax.ppermute(down, "seq", above))
            arrays.append([owns[g], ups[g], downs[g]])
            if far:
                up, down = ups[g][half:], downs[g][:half]
                if g == last_group:
                    for earlier in range(1):
                        meet(earlier)
                    up, down = after(up, *met), after(down, *met)
                arrays[g] += [lax.ppermute(up, "seq", below), lax.ppermute(down, "seq", above)]
        for g in range(len(met), len(GROUPS)):
            meet(g)
        outputs = []
        for array in met[-2:]:
            returned = exchange(array.reshape(parties, piece, -1))
            outputs.append(jnp.transpose(returned, (1, 0, 2)).reshape(piece, -1))
        return jnp.concatenate(outputs, axis=1)

    operands = (first_own, key_packs[1:], query_pack, frame)
    near_only = functools.partial(finish, far=False)
    if planes < 3:
        return near_only(*operands)
    bounding = segment_ids.reshape(planes, plane_rows)
    crossed = jnp.any(bounding[:-2, -1] == bounding[2:, 0])
    return lax.cond(crossed, functools.partial(finish, far=True), near_only, *operands)


def solution(mesh):
    placed = (
        P(None, ("seq", "head"), None),
        P(None, ("seq", "head"), None),
        P(None, ("seq", "head"), None),
        P(),
        P(),
        P(),
        P(),
    )
    return jax.shard_map(
        on_device, mesh=mesh, in_specs=placed, out_specs=P(("seq", "head"), None), check_vma=False
    )
```

```python
import functools
import math

import jax
import jax.numpy as jnp
from jax import lax
from jax.experimental import pallas as pl
from jax.experimental.pallas import tpu as pltpu
from jax.sharding import PartitionSpec as P

HEAD_DIM = 128
REACH = 3
PAIR = 2
GROUPS = (2, 2, 1)
RETURNS = ((0,), (1, 2))
TILE_KEYS = 1280

guide_denominator = 4.0
norm_epsilon = 1e-06
masked_score = -1e30
score_scale = HEAD_DIM ** (-0.5) * math.log2(math.e)
AXES = ("seq", "head")


def group_ranges(total):
    first, ranges = 0, []
    for count in GROUPS:
        ranges.append((first, count))
        first += count
    assert first == total
    return ranges


def return_of(group):
    for together in RETURNS:
        if group in together:
            return sum(GROUPS[: together[0]]), sum(GROUPS[g] for g in together)


def first_feature(group, party, parties):
    first, count = return_of(group)
    own = sum(GROUPS[:group]) - first
    return (first * parties + party * count + own) * HEAD_DIM


def normed(raw_rows, gain):
    widened = raw_rows.astype(jnp.float32)
    mean_square = jnp.mean(widened * widened, axis=-1, keepdims=True)
    return (widened * lax.rsqrt(mean_square + norm_epsilon) * gain).astype(jnp.bfloat16)


def scatter_heads(rows, out_refs, slot, parties):
    for group, ref in enumerate(out_refs):
        for party in range(parties):
            begin = first_feature(group, party, parties)
            ref[party, slot, 0] = rows[:, begin : begin + ref.shape[-1]]


def pack_keys_body(key_ref, value_ref, gain_ref, *out_refs, parties):
    scatter_heads(normed(key_ref[0], gain_ref[...]), out_refs, 0, parties)
    scatter_heads(value_ref[0], out_refs, 1, parties)


def pack_queries_body(query_ref, gain_ref, out_ref, *, parties):
    rows = normed(query_ref[0], gain_ref[...])
    for group, (first, count) in enumerate(group_ranges(out_ref.shape[-1] // HEAD_DIM)):
        columns = slice(first * HEAD_DIM, (first + count) * HEAD_DIM)
        for party in range(parties):
            begin = first_feature(group, party, parties)
            out_ref[party, 0, :, columns] = rows[:, begin : begin + count * HEAD_DIM]


def pack(body, arrays, gain, parties, slots, ranges):
    branches, row_count, width = arrays[0].shape
    half = row_count // 2
    row_spec = pl.BlockSpec((1, half, width), lambda b, r: (b, r, 0))
    out_shape, out_specs = [], []
    for _, count in ranges:
        own = count * HEAD_DIM
        lead = (parties,) + slots
        out_shape.append(jax.ShapeDtypeStruct(lead + (branches, row_count, own), jnp.bfloat16))
        zeros = (0,) * len(lead)
        out_specs.append(
            pl.BlockSpec(lead + (1, half, own), lambda b, r, zeros=zeros: zeros + (b, r, 0))
        )
    return pl.pallas_call(
        functools.partial(body, parties=parties),
        grid=(branches, 2),
        in_specs=[row_spec] * len(arrays) + [pl.BlockSpec((1, width), lambda b, r: (0, 0))],
        out_specs=out_specs,
        out_shape=out_shape,
        compiler_params=pltpu.CompilerParams(vmem_limit_bytes=48 << 20),
    )(*arrays, gain.reshape(1, width))


def attend_body(bounds_ref, query_ref, *refs, chunks, chunk_refs, tile_rows, tile_keys):
    chunk_arrays = refs[:chunk_refs]
    key_segments, query_segments, scale_ref = refs[chunk_refs : chunk_refs + 3]
    out_ref, query_rows, key_rows, value_rows, max_ref, sum_ref, acc_ref = refs[-7:]
    parties, branches, piece, _ = query_ref.shape
    plane_rows = parties * piece
    tiles = plane_rows // tile_rows
    every = range(branches)
    lowest = bounds_ref[0]
    beyond = bounds_ref[2 * tiles - 1]

    @pl.when(pl.program_id(0) == 0)
    def _():
        value_rows[...] = jnp.zeros(value_rows.shape, value_rows.dtype)

    for b in every:
        query_rows[b] = query_ref[:, b].reshape(plane_rows, HEAD_DIM)
    for which, begin, pieces, offset in chunks:
        rows = pieces * piece
        first = offset * piece

        @pl.when(jnp.logical_and(first < beyond, first + rows > lowest))
        def _():
            for b in every:
                here = chunk_arrays[which][begin : begin + pieces, :, b]
                key_rows[b, first : first + rows] = here[:, 0].reshape(rows, HEAD_DIM)
                value_rows[b, first : first + rows] = here[:, 1].reshape(rows, HEAD_DIM)

    def attend_tile(t, _):
        at = pl.ds(pl.multiple_of(t * tile_rows, tile_rows), tile_rows)
        start = bounds_ref[2 * t] // HEAD_DIM * HEAD_DIM
        count = (bounds_ref[2 * t + 1] - start + tile_keys - 1) // tile_keys
        own_segments = query_segments[at]
        queries = [query_rows[b, at] for b in every]
        for b in every:
            max_ref[b] = jnp.full((tile_rows, HEAD_DIM), masked_score, jnp.float32)
            sum_ref[b] = jnp.zeros((tile_rows, HEAD_DIM), jnp.float32)
            acc_ref[b] = jnp.zeros((tile_rows, HEAD_DIM), jnp.float32)

        def absorb(k, _):
            here = pl.ds(pl.multiple_of(start + k * tile_keys, HEAD_DIM), tile_keys)
            copies = tile_keys // HEAD_DIM
            same = jnp.concatenate([own_segments] * copies, axis=1) == key_segments[:, here]
            old = [max_ref[b] for b in every]
            sums = [sum_ref[b] for b in every]
            weighted = [acc_ref[b] for b in every]
            keys = [key_rows[b, here] for b in every]
            values = [value_rows[b, here] for b in every]
            scores = [
                lax.dot_general(
                    queries[b], keys[b], (((1,), (1,)), ((), ())), preferred_element_type=jnp.float32
                )
                for b in every
            ]
            scores = [jnp.where(same, scores[b] * score_scale, masked_score) for b in every]
            highest = [
                jnp.maximum(old[b], jnp.max(scores[b], axis=1, keepdims=True)) for b in every
            ]
            factor = [jnp.exp2(old[b] - highest[b]) for b in every]
            exponents = [
                jnp.exp2(scores[b] - jnp.concatenate([highest[b]] * copies, axis=1)) for b in every
            ]
            partial = []
            for b in every:
                lanes = exponents[b][:, :HEAD_DIM]
                for i in range(1, copies):
                    lanes = lanes + exponents[b][:, i * HEAD_DIM : (i + 1) * HEAD_DIM]
                partial.append(lanes)
            products = [
                jnp.dot(
                    exponents[b].astype(jnp.bfloat16), values[b], preferred_element_type=jnp.float32
                )
                for b in every
            ]
            for b in every:
                max_ref[b] = highest[b]
                sum_ref[b] = sums[b] * factor[b] + partial[b]
                acc_ref[b] = weighted[b] * factor[b] + products[b]
            return 0

        lax.fori_loop(0, count, absorb, 0)
        attended = [
            (acc_ref[b] / jnp.sum(sum_ref[b], axis=1, keepdims=True))
            .astype(jnp.bfloat16)
            .astype(jnp.float32)
            for b in every
        ]
        guided = attended[1] + scale_ref[at] * (attended[0] - attended[1])
        out_ref[at] = guided.astype(jnp.bfloat16)
        return 0

    lax.fori_loop(0, tiles, attend_tile, 0)


def attend(queries, first_head, key_arrays, chunks, frame, out_heads, out_first, into):
    bounds, key_segments, query_segments, row_scale = frame
    parties, branches, piece, _ = queries.shape
    width = key_arrays[0].shape[-1]
    plane_rows = parties * piece
    tiles = bounds.shape[0] // 2
    window_rows = key_segments.shape[1]

    def head_spec(array, skip):
        return pl.BlockSpec(
            array.shape[:-1] + (HEAD_DIM,),
            lambda h, _, n=array.ndim, skip=skip: (0,) * (n - 1) + (h + skip,),
        )

    def whole_spec(array):
        return pl.BlockSpec(array.shape, lambda h, _, n=array.ndim: (0,) * n)

    tile_rows = plane_rows // tiles
    return pl.pallas_call(
        functools.partial(
            attend_body,
            chunks=chunks,
            chunk_refs=len(key_arrays),
            tile_rows=tile_rows,
            tile_keys=TILE_KEYS,
        ),
        grid_spec=pltpu.PrefetchScalarGridSpec(
            num_scalar_prefetch=1,
            grid=(width // HEAD_DIM,),
            in_specs=[head_spec(queries, first_head)]
            + [head_spec(array, 0) for array in key_arrays]
            + [whole_spec(key_segments), whole_spec(query_segments), whole_spec(row_scale)]
            + [pl.BlockSpec(memory_space=pl.ANY)] * len(into),
            out_specs=pl.BlockSpec((plane_rows, HEAD_DIM), lambda h, _: (0, h + out_first)),
            scratch_shapes=[
                pltpu.VMEM((branches, plane_rows, HEAD_DIM), jnp.bfloat16),
                pltpu.VMEM((branches, window_rows, HEAD_DIM), jnp.bfloat16),
                pltpu.VMEM((branches, window_rows, HEAD_DIM), jnp.bfloat16),
                pltpu.VMEM((branches, tile_rows, HEAD_DIM), jnp.float32),
                pltpu.VMEM((branches, tile_rows, HEAD_DIM), jnp.float32),
                pltpu.VMEM((branches, tile_rows, HEAD_DIM), jnp.float32),
            ],
        ),
        out_shape=jax.ShapeDtypeStruct((plane_rows, out_heads * HEAD_DIM), jnp.bfloat16),
        input_output_aliases={5 + len(key_arrays): 0} if into else {},
        compiler_params=pltpu.CompilerParams(vmem_limit_bytes=48 << 20),
        cost_estimate=pl.CostEstimate(
            flops=4 * branches * plane_rows * plane_rows * width,
            transcendentals=branches * plane_rows * plane_rows * width // HEAD_DIM,
            bytes_accessed=4 * branches * plane_rows * width * 2,
        ),
    )(bounds, queries, *key_arrays, key_segments, query_segments, row_scale, *into)


def guide_rows(row_segments, guidance):
    clip_count = guidance.shape[0]
    one_hot = (row_segments[:, None] == jnp.arange(clip_count, dtype=jnp.int32)[None, :]).astype(
        jnp.float32
    )
    return (
        jnp.dot(one_hot, guidance.astype(jnp.float32), precision=lax.Precision.HIGHEST)
        / guide_denominator
    )


def after(value, *gates):
    return lax.optimization_barrier((value,) + gates)[0]


def on_device(query_rows, key_rows, value_rows, segment_ids, query_gain, key_gain, guidance):
    seq_count = lax.axis_size("seq")
    head_groups = lax.axis_size("head")
    parties = PAIR * head_groups
    planes = seq_count // PAIR
    plane = lax.axis_index("seq") // PAIR
    branches, piece, width = query_rows.shape
    plane_rows = parties * piece
    margin = REACH * head_groups * piece
    window_rows = plane_rows + 2 * margin
    half = head_groups

    rows = jnp.arange(window_rows + TILE_KEYS, dtype=jnp.int32) + (plane * plane_rows - margin)
    padded = jnp.pad(segment_ids, (margin, margin + TILE_KEYS))
    window = lax.dynamic_slice_in_dim(padded, plane * plane_rows, window_rows + TILE_KEYS)
    window = jnp.where(rows < 0, -1, jnp.where(rows < segment_ids.shape[0], window, guidance.shape[0]))
    own_segments = lax.dynamic_slice_in_dim(segment_ids, plane * plane_rows, plane_rows)
    row_scale = jnp.broadcast_to(guide_rows(own_segments, guidance)[:, None], (plane_rows, HEAD_DIM))
    tile_segments = own_segments.reshape(PAIR, plane_rows // PAIR)
    ends = jnp.stack([tile_segments[:, 0] - 1, tile_segments[:, -1]], axis=1).reshape(-1, 1)
    bounds = jnp.sum((window[None, :] <= ends).astype(jnp.int32), axis=1)
    frame = (
        bounds,
        window[None, :],
        jnp.broadcast_to(own_segments[:, None], (plane_rows, HEAD_DIM)),
        row_scale,
    )

    chunks = (
        (0, 0, parties, 3 * half),
        (1, 0, parties, half),
        (2, 0, parties, 5 * half),
        (3, 0, half, 0),
        (4, 0, half, 7 * half),
    )
    planes_of = [
        [plane_at * parties + member for member in range(parties)] for plane_at in range(planes)
    ]
    below = [(s, s + PAIR) for s in range(seq_count - PAIR)]
    above = [(s + PAIR, s) for s in range(seq_count - PAIR)]

    def exchange(array):
        return lax.all_to_all(array, AXES, 0, 0, axis_index_groups=planes_of, tiled=True)

    heads = width // HEAD_DIM // parties
    ranges = group_ranges(heads)
    key_packs = pack(pack_keys_body, (key_rows, value_rows), key_gain, parties, (2,), ranges)
    (query_pack,) = pack(pack_queries_body, (query_rows,), query_gain, parties, (), [(0, heads)])
    first_own = exchange(key_packs[0])
    last_group = len(GROUPS) - 1

    def finish(own, later_packs, query_pack, frame, far):
        owns, ups, downs, arrays, met, returned = [own], [], [], [], [], []
        queries = None

        def meet(g):
            first, count = ranges[g]
            out_first, out_heads = return_of(g)
            into = met[-1:] if first > out_first else []
            met.append(
                attend(
                    queries, first, arrays[g], chunks[: len(arrays[g])], frame,
                    out_heads, first - out_first, into,
                )
            )
            if first + count == out_first + out_heads:
                returned.append(exchange(met[-1].reshape(parties, piece, -1)))

        for g in range(len(GROUPS)):
            if g == 1:
                owns.append(exchange(later_packs[0]))
                queries = exchange(after(query_pack, owns[1]))
            elif g > 1:
                owns.append(exchange(after(later_packs[g - 1], queries)))
            up = down = owns[g]
            if g == last_group:
                meet(0)
            if g == 1:
                up, down = after(up, ups[0]), after(down, downs[0])
            if g == 2 and not far:
                up, down = after(up, *met), after(down, *met)
            if g == 2 and far:
                up, down = after(up, ups[1]), after(down, downs[1])
            ups.append(lax.ppermute(up, "seq", below))
            downs.append(lax.ppermute(down, "seq", above))
            arrays.append([owns[g], ups[g], downs[g]])
            if far:
                up, down = ups[g][half:], downs[g][:half]
                if g == last_group:
                    for earlier in range(1, 1):
                        meet(earlier)
                    up, down = after(up, *met), after(down, *met)
                arrays[g] += [lax.ppermute(up, "seq", below), lax.ppermute(down, "seq", above)]
        for g in range(len(met), len(GROUPS)):
            meet(g)
        outputs = [jnp.transpose(array, (1, 0, 2)).reshape(piece, -1) for array in returned]
        return jnp.concatenate(outputs, axis=1)

    operands = (first_own, key_packs[1:], query_pack, frame)
    near_only = functools.partial(finish, far=False)
    if planes < 3:
        return near_only(*operands)
    bounding = segment_ids.reshape(planes, plane_rows)
    crossed = jnp.any(bounding[:-2, -1] == bounding[2:, 0])
    return lax.cond(crossed, functools.partial(finish, far=True), near_only, *operands)


def solution(mesh):
    placed = (
        P(None, ("seq", "head"), None),
        P(None, ("seq", "head"), None),
        P(None, ("seq", "head"), None),
        P(),
        P(),
        P(),
        P(),
    )
    return jax.shard_map(
        on_device, mesh=mesh, in_specs=placed, out_specs=P(("seq", "head"), None), check_vma=False
    )
```

```python
import functools
import math

import jax
import jax.numpy as jnp
from jax import lax
from jax.experimental import pallas as pl
from jax.experimental.pallas import tpu as pltpu
from jax.sharding import PartitionSpec as P

HEAD_DIM = 128
REACH = 3
PAIR = 2
GROUPS = (2, 2, 1)
RETURNS = ((0,), (1, 2))
TILE_KEYS = 1280

guide_denominator = 4.0
norm_epsilon = 1e-06
masked_score = -1e30
score_scale = HEAD_DIM ** (-0.5) * math.log2(math.e)
AXES = ("seq", "head")


def group_ranges(total):
    first, ranges = 0, []
    for count in GROUPS:
        ranges.append((first, count))
        first += count
    assert first == total
    return ranges


def return_of(group):
    for together in RETURNS:
        if group in together:
            return sum(GROUPS[: together[0]]), sum(GROUPS[g] for g in together)


def first_feature(group, party, parties):
    first, count = return_of(group)
    own = sum(GROUPS[:group]) - first
    return (first * parties + party * count + own) * HEAD_DIM


def normed(raw_rows, gain):
    widened = raw_rows.astype(jnp.float32)
    mean_square = jnp.mean(widened * widened, axis=-1, keepdims=True)
    return (widened * lax.rsqrt(mean_square + norm_epsilon) * gain).astype(jnp.bfloat16)


def scatter_heads(rows, out_refs, slot, parties):
    for group, ref in enumerate(out_refs):
        for party in range(parties):
            begin = first_feature(group, party, parties)
            ref[party, slot, 0] = rows[:, begin : begin + ref.shape[-1]]


def pack_keys_body(key_ref, value_ref, gain_ref, *out_refs, parties):
    scatter_heads(normed(key_ref[0], gain_ref[...]), out_refs, 0, parties)
    scatter_heads(value_ref[0], out_refs, 1, parties)


def pack_queries_body(query_ref, gain_ref, out_ref, *, parties):
    rows = normed(query_ref[0], gain_ref[...])
    for group, (first, count) in enumerate(group_ranges(out_ref.shape[-1] // HEAD_DIM)):
        columns = slice(first * HEAD_DIM, (first + count) * HEAD_DIM)
        for party in range(parties):
            begin = first_feature(group, party, parties)
            out_ref[party, 0, :, columns] = rows[:, begin : begin + count * HEAD_DIM]


def pack(body, arrays, gain, parties, slots, ranges):
    branches, row_count, width = arrays[0].shape
    row_spec = pl.BlockSpec((1, row_count, width), lambda b: (b, 0, 0))
    out_shape, out_specs = [], []
    for _, count in ranges:
        own = count * HEAD_DIM
        lead = (parties,) + slots
        out_shape.append(jax.ShapeDtypeStruct(lead + (branches, row_count, own), jnp.bfloat16))
        zeros = (0,) * len(lead)
        out_specs.append(
            pl.BlockSpec(lead + (1, row_count, own), lambda b, zeros=zeros: zeros + (b, 0, 0))
        )
    return pl.pallas_call(
        functools.partial(body, parties=parties),
        grid=(branches,),
        in_specs=[row_spec] * len(arrays) + [pl.BlockSpec((1, width), lambda b: (0, 0))],
        out_specs=out_specs,
        out_shape=out_shape,
        compiler_params=pltpu.CompilerParams(vmem_limit_bytes=48 << 20),
    )(
        *[pltpu.with_memory_space_constraint(array, pltpu.HBM) for array in arrays],
        gain.reshape(1, width),
    )


def attend_body(bounds_ref, query_ref, *refs, chunks, chunk_refs, tile_rows, tile_keys):
    chunk_arrays = refs[:chunk_refs]
    key_segments, query_segments, scale_ref = refs[chunk_refs : chunk_refs + 3]
    out_ref, query_rows, key_rows, value_rows, max_ref, sum_ref, acc_ref = refs[-7:]
    parties, branches, piece, _ = query_ref.shape
    plane_rows = parties * piece
    tiles = plane_rows // tile_rows
    every = range(branches)
    lowest = bounds_ref[0]
    beyond = bounds_ref[2 * tiles - 1]

    @pl.when(pl.program_id(0) == 0)
    def _():
        value_rows[...] = jnp.zeros(value_rows.shape, value_rows.dtype)

    for b in every:
        query_rows[b] = query_ref[:, b].reshape(plane_rows, HEAD_DIM)
    for which, begin, pieces, offset in chunks:
        rows = pieces * piece
        first = offset * piece

        @pl.when(jnp.logical_and(first < beyond, first + rows > lowest))
        def _():
            for b in every:
                here = chunk_arrays[which][begin : begin + pieces, :, b]
                key_rows[b, first : first + rows] = here[:, 0].reshape(rows, HEAD_DIM)
                value_rows[b, first : first + rows] = here[:, 1].reshape(rows, HEAD_DIM)

    def attend_tile(t, _):
        at = pl.ds(pl.multiple_of(t * tile_rows, tile_rows), tile_rows)
        start = bounds_ref[2 * t] // HEAD_DIM * HEAD_DIM
        count = (bounds_ref[2 * t + 1] - start + tile_keys - 1) // tile_keys
        own_segments = query_segments[at]
        queries = [query_rows[b, at] for b in every]
        for b in every:
            max_ref[b] = jnp.full((tile_rows, HEAD_DIM), masked_score, jnp.float32)
            sum_ref[b] = jnp.zeros((tile_rows, HEAD_DIM), jnp.float32)
            acc_ref[b] = jnp.zeros((tile_rows, HEAD_DIM), jnp.float32)

        def absorb(k, _):
            here = pl.ds(pl.multiple_of(start + k * tile_keys, HEAD_DIM), tile_keys)
            copies = tile_keys // HEAD_DIM
            same = jnp.concatenate([own_segments] * copies, axis=1) == key_segments[:, here]
            old = [max_ref[b] for b in every]
            sums = [sum_ref[b] for b in every]
            weighted = [acc_ref[b] for b in every]
            keys = [key_rows[b, here] for b in every]
            values = [value_rows[b, here] for b in every]
            scores = [
                lax.dot_general(
                    queries[b], keys[b], (((1,), (1,)), ((), ())), preferred_element_type=jnp.float32
                )
                for b in every
            ]
            scores = [jnp.where(same, scores[b] * score_scale, masked_score) for b in every]
            highest = [
                jnp.maximum(old[b], jnp.max(scores[b], axis=1, keepdims=True)) for b in every
            ]
            factor = [jnp.exp2(old[b] - highest[b]) for b in every]
            exponents = [
                jnp.exp2(scores[b] - jnp.concatenate([highest[b]] * copies, axis=1)) for b in every
            ]
            partial = []
            for b in every:
                lanes = exponents[b][:, :HEAD_DIM]
                for i in range(1, copies):
                    lanes = lanes + exponents[b][:, i * HEAD_DIM : (i + 1) * HEAD_DIM]
                partial.append(lanes)
            products = [
                jnp.dot(
                    exponents[b].astype(jnp.bfloat16), values[b], preferred_element_type=jnp.float32
                )
                for b in every
            ]
            for b in every:
                max_ref[b] = highest[b]
                sum_ref[b] = sums[b] * factor[b] + partial[b]
                acc_ref[b] = weighted[b] * factor[b] + products[b]
            return 0

        lax.fori_loop(0, count, absorb, 0)
        attended = [
            (acc_ref[b] / jnp.sum(sum_ref[b], axis=1, keepdims=True))
            .astype(jnp.bfloat16)
            .astype(jnp.float32)
            for b in every
        ]
        guided = attended[1] + scale_ref[at] * (attended[0] - attended[1])
        out_ref[at] = guided.astype(jnp.bfloat16)
        return 0

    lax.fori_loop(0, tiles, attend_tile, 0)


def attend(queries, first_head, key_arrays, chunks, frame, out_heads, out_first, into):
    bounds, key_segments, query_segments, row_scale = frame
    parties, branches, piece, _ = queries.shape
    width = key_arrays[0].shape[-1]
    plane_rows = parties * piece
    tiles = bounds.shape[0] // 2
    window_rows = key_segments.shape[1]

    def head_spec(array, skip):
        return pl.BlockSpec(
            array.shape[:-1] + (HEAD_DIM,),
            lambda h, _, n=array.ndim, skip=skip: (0,) * (n - 1) + (h + skip,),
        )

    def whole_spec(array):
        return pl.BlockSpec(array.shape, lambda h, _, n=array.ndim: (0,) * n)

    tile_rows = plane_rows // tiles
    return pl.pallas_call(
        functools.partial(
            attend_body,
            chunks=chunks,
            chunk_refs=len(key_arrays),
            tile_rows=tile_rows,
            tile_keys=TILE_KEYS,
        ),
        grid_spec=pltpu.PrefetchScalarGridSpec(
            num_scalar_prefetch=1,
            grid=(width // HEAD_DIM,),
            in_specs=[head_spec(queries, first_head)]
            + [head_spec(array, 0) for array in key_arrays]
            + [whole_spec(key_segments), whole_spec(query_segments), whole_spec(row_scale)]
            + [pl.BlockSpec(memory_space=pl.ANY)] * len(into),
            out_specs=pl.BlockSpec((plane_rows, HEAD_DIM), lambda h, _: (0, h + out_first)),
            scratch_shapes=[
                pltpu.VMEM((branches, plane_rows, HEAD_DIM), jnp.bfloat16),
                pltpu.VMEM((branches, window_rows, HEAD_DIM), jnp.bfloat16),
                pltpu.VMEM((branches, window_rows, HEAD_DIM), jnp.bfloat16),
                pltpu.VMEM((branches, tile_rows, HEAD_DIM), jnp.float32),
                pltpu.VMEM((branches, tile_rows, HEAD_DIM), jnp.float32),
                pltpu.VMEM((branches, tile_rows, HEAD_DIM), jnp.float32),
            ],
        ),
        out_shape=jax.ShapeDtypeStruct((plane_rows, out_heads * HEAD_DIM), jnp.bfloat16),
        input_output_aliases={5 + len(key_arrays): 0} if into else {},
        compiler_params=pltpu.CompilerParams(vmem_limit_bytes=48 << 20),
        cost_estimate=pl.CostEstimate(
            flops=4 * branches * plane_rows * plane_rows * width,
            transcendentals=branches * plane_rows * plane_rows * width // HEAD_DIM,
            bytes_accessed=4 * branches * plane_rows * width * 2,
        ),
    )(bounds, queries, *key_arrays, key_segments, query_segments, row_scale, *into)


def guide_rows(row_segments, guidance):
    clip_count = guidance.shape[0]
    one_hot = (row_segments[:, None] == jnp.arange(clip_count, dtype=jnp.int32)[None, :]).astype(
        jnp.float32
    )
    return (
        jnp.dot(one_hot, guidance.astype(jnp.float32), precision=lax.Precision.HIGHEST)
        / guide_denominator
    )


def after(value, *gates):
    return lax.optimization_barrier((value,) + gates)[0]


def on_device(query_rows, key_rows, value_rows, segment_ids, query_gain, key_gain, guidance):
    seq_count = lax.axis_size("seq")
    head_groups = lax.axis_size("head")
    parties = PAIR * head_groups
    planes = seq_count // PAIR
    plane = lax.axis_index("seq") // PAIR
    branches, piece, width = query_rows.shape
    plane_rows = parties * piece
    margin = REACH * head_groups * piece
    window_rows = plane_rows + 2 * margin
    half = head_groups

    rows = jnp.arange(window_rows + TILE_KEYS, dtype=jnp.int32) + (plane * plane_rows - margin)
    padded = jnp.pad(segment_ids, (margin, margin + TILE_KEYS))
    window = lax.dynamic_slice_in_dim(padded, plane * plane_rows, window_rows + TILE_KEYS)
    window = jnp.where(rows < 0, -1, jnp.where(rows < segment_ids.shape[0], window, guidance.shape[0]))
    own_segments = lax.dynamic_slice_in_dim(segment_ids, plane * plane_rows, plane_rows)
    row_scale = jnp.broadcast_to(guide_rows(own_segments, guidance)[:, None], (plane_rows, HEAD_DIM))
    tile_segments = own_segments.reshape(PAIR, plane_rows // PAIR)
    ends = jnp.stack([tile_segments[:, 0] - 1, tile_segments[:, -1]], axis=1).reshape(-1, 1)
    bounds = jnp.sum((window[None, :] <= ends).astype(jnp.int32), axis=1)
    frame = (
        bounds,
        window[None, :],
        jnp.broadcast_to(own_segments[:, None], (plane_rows, HEAD_DIM)),
        row_scale,
    )

    chunks = (
        (0, 0, parties, 3 * half),
        (1, 0, parties, half),
        (2, 0, parties, 5 * half),
        (3, 0, half, 0),
        (4, 0, half, 7 * half),
    )
    planes_of = [
        [plane_at * parties + member for member in range(parties)] for plane_at in range(planes)
    ]
    below = [(s, s + PAIR) for s in range(seq_count - PAIR)]
    above = [(s + PAIR, s) for s in range(seq_count - PAIR)]

    def exchange(array):
        return lax.all_to_all(array, AXES, 0, 0, axis_index_groups=planes_of, tiled=True)

    heads = width // HEAD_DIM // parties
    ranges = group_ranges(heads)
    key_packs = pack(pack_keys_body, (key_rows, value_rows), key_gain, parties, (2,), ranges)
    (query_pack,) = pack(pack_queries_body, (query_rows,), query_gain, parties, (), [(0, heads)])
    first_own = exchange(key_packs[0])
    last_group = len(GROUPS) - 1

    def finish(own, later_packs, query_pack, frame, far):
        owns, ups, downs, arrays, met, returned = [own], [], [], [], [], []
        queries = None

        def meet(g):
            first, count = ranges[g]
            out_first, out_heads = return_of(g)
            into = met[-1:] if first > out_first else []
            met.append(
                attend(
                    queries, first, arrays[g], chunks[: len(arrays[g])], frame,
                    out_heads, first - out_first, into,
                )
            )
            if first + count == out_first + out_heads:
                returned.append(exchange(met[-1].reshape(parties, piece, -1)))

        for g in range(len(GROUPS)):
            if g == 1:
                owns.append(exchange(later_packs[0]))
                queries = exchange(after(query_pack, owns[1]))
            elif g > 1:
                owns.append(exchange(after(later_packs[g - 1], queries)))
            up = down = owns[g]
            if g == last_group:
                meet(0)
            if g == 1:
                up, down = after(up, ups[0]), after(down, downs[0])
            if g == 2 and not far:
                up, down = after(up, *met), after(down, *met)
            if g == 2 and far:
                up, down = after(up, ups[1]), after(down, downs[1])
            ups.append(lax.ppermute(up, "seq", below))
            downs.append(lax.ppermute(down, "seq", above))
            arrays.append([owns[g], ups[g], downs[g]])
            if far:
                up, down = ups[g][half:], downs[g][:half]
                if g == last_group:
                    for earlier in range(1, 1):
                        meet(earlier)
                    up, down = after(up, *met), after(down, *met)
                arrays[g] += [lax.ppermute(up, "seq", below), lax.ppermute(down, "seq", above)]
        for g in range(len(met), len(GROUPS)):
            meet(g)
        outputs = [jnp.transpose(array, (1, 0, 2)).reshape(piece, -1) for array in returned]
        return jnp.concatenate(outputs, axis=1)

    operands = (first_own, key_packs[1:], query_pack, frame)
    near_only = functools.partial(finish, far=False)
    if planes < 3:
        return near_only(*operands)
    bounding = segment_ids.reshape(planes, plane_rows)
    crossed = jnp.any(bounding[:-2, -1] == bounding[2:, 0])
    return lax.cond(crossed, functools.partial(finish, far=True), near_only, *operands)


def solution(mesh):
    placed = (
        P(None, ("seq", "head"), None),
        P(None, ("seq", "head"), None),
        P(None, ("seq", "head"), None),
        P(),
        P(),
        P(),
        P(),
    )
    return jax.shard_map(
        on_device, mesh=mesh, in_specs=placed, out_specs=P(("seq", "head"), None), check_vma=False
    )
```
